1024 devices in a mesh: tm: 32 (over z, core), space: 4 (over x), node: 8 (over y).
Axes of the slice: x: 4, y: 8, z: 16, core: 2. Of those that a mesh axis runs over, the one named last changes fastest.
Arguments:
- initial: float32 [8, 64, 256], P(None, 'space'), may hold values from -6 to 6
- forcing: float32 [32, 8, 64, 256], P('tm', None, 'space'), may hold values from -6 to 6
- decay_rate: float32 [8, 64, 256], P(None, 'space'), may hold values from 0.02 to 20
- mixing: float32 [8, 8], replicated, may hold values from -2 to 2
- diffusivity: float32 [8], replicated, may hold values from 0.3 to 2
- velocity: float32 [3, 8], replicated, may hold values from -2 to 2
Outputs:
- node_values: float32 [32, 8, 8, 64, 256], P('tm', 'node', None, 'space')
The draws below stay inside these ranges and needn't reach their ends.
All inputs are finite; a program needn't handle non-finite values.
Results may differ from the reference program's by a relative error of at most 0.0003.
Values sent between devices are 32-bit elements; how exact they have to be, the bound alone decides.
No kernel may reach another device: no remote copies, remote signals or barrier semaphores. Data moves between devices by JAX's collectives and lax.ppermute only.
A program may use at most 32 MiB of HBM per device.

```python
import math
import jax
import jax.numpy as jnp
import numpy as np
from jax import lax

S = 8
NY = 16
NZ = 16
NX = 64
SLICES = 32
N_NODE = 8


def shard_levels(key, shape, pieces, least, top_value):
    loudness = 1.0
    for dim, parts in pieces:
        draws = jax.random.uniform(jax.random.fold_in(jax.random.fold_in(key, 6), dim), (parts,), jnp.float32, least / len(pieces), top_value / len(pieces))
        loudness = loudness * jnp.repeat(jnp.exp(draws), shape[dim] // parts).reshape((-1,) + (1,) * (len(shape) - 1 - dim))
    return loudness


def gaussian(rng, shape, deviation, reach, split=(), dtype=jnp.bfloat16):
    entries = jax.random.normal(rng, shape, jnp.float32) * deviation
    if len(split) > 0:
        entries = shard_levels(rng, shape, split, -0.22, 0.18) * entries
    return jnp.clip(entries, min=-reach, max=reach).astype(dtype)


def setup_inputs(seed: int = 0) -> dict:
    streams_of = jax.random.split(jax.random.key(seed), 7)
    initial = gaussian(streams_of[0], (S, NX, NY * NZ), 1.0, 6.0, ((1, 4),), jnp.float32)
    forcing = gaussian(streams_of[1], (SLICES, S, NX, NY * NZ), 1.0, 6.0, ((0, 32), (2, 4)), jnp.float32)
    decay_rate = jnp.clip(jnp.exp(math.log(20.0) - 6.9077553 * jax.random.uniform(streams_of[2], (S, NX, NY * NZ), jnp.float32) ** shard_levels(streams_of[2], (S, NX, NY * NZ), ((1, 4),), -0.2, 0.2)), 0.02, 20.0)
    mixing = gaussian(streams_of[3], (S, S), S ** -0.5, 2.0, (), jnp.float32)
    diffusivity = jnp.clip(jnp.exp(jax.random.uniform(streams_of[4], (S,), jnp.float32, math.log(0.3), math.log(2.0))), 0.3, 2.0)
    velocity = jnp.clip(jax.random.uniform(streams_of[5], (3, S), jnp.float32, -2.0, 2.0), -2.0, 2.0)
    return dict(initial=initial, forcing=forcing, decay_rate=decay_rate, mixing=mixing, diffusivity=diffusivity, velocity=velocity)


time_step = 0.05


def quadrature(node_count):
    points = [(position + 1.0) / node_count for position in range(node_count)]
    weights_table = np.zeros((node_count, node_count))
    for column in range(node_count):
        coeffs = [1.0]
        denominator = 1.0
        for other_node in range(node_count):
            if other_node != column:
                shifted = [0.0] + coeffs
                for degree in range(len(coeffs)):
                    shifted[degree] = shifted[degree] - points[other_node] * coeffs[degree]
                coeffs = shifted
                denominator = denominator * (points[column] - points[other_node])
        for row_node in range(node_count):
            running = 0.0
            for degree in range(len(coeffs)):
                running = running + coeffs[degree] * points[row_node] ** (degree + 1) / (degree + 1)
            weights_table[row_node, column] = running / denominator
    return weights_table, np.array(points)


def rate_of(padded, decay_rate, mixing, diffusivity, velocity, force_now):
    center = padded[:, 1:-1]
    x_plus = padded[:, 2:]
    x_minus = padded[:, :-2]
    y_plus = jnp.roll(center, -NZ, axis=2)
    y_minus = jnp.roll(center, NZ, axis=2)
    depth_index = jnp.arange(center.shape[2]) % NZ
    z_plus = jnp.where(depth_index == NZ - 1, 0.0, jnp.roll(center, -1, axis=2))
    z_minus = jnp.where(depth_index == 0, 0.0, jnp.roll(center, 1, axis=2))
    laplace = (x_plus + x_minus) + (y_plus + y_minus) + (z_plus + z_minus) - 6.0 * center
    drift_term = (velocity[0][:, None, None] * (x_plus - x_minus)
                  + velocity[1][:, None, None] * (y_plus - y_minus)
                  + velocity[2][:, None, None] * (z_plus - z_minus))
    coupled = jnp.tanh(jnp.einsum("ts,sxc->txc", mixing, center, precision=lax.Precision.HIGHEST))
    return diffusivity[:, None, None] * laplace - 0.5 * drift_term - decay_rate * center + coupled + force_now


def reference(initial, forcing, decay_rate, mixing, diffusivity, velocity):
    weights_table, points = quadrature(N_NODE)
    q_table = jnp.asarray(weights_table, jnp.float32)
    node_time = jnp.asarray(points, jnp.float32)[:, None, None, None]
    stiff_part = time_step * (node_time / N_NODE) * decay_rate[None]
    factor = 1.0 / (1.0 + time_step * decay_rate)

    def advance(carried, force_now):
        return factor * carried + time_step * force_now * factor, carried

    _, starts = lax.scan(advance, initial, forcing)

    def first_nodes(slice_start, force_now):
        return (slice_start[None] + node_time * time_step * force_now[None]) / (1.0 + node_time * time_step * decay_rate[None])

    def sweep_nodes(slice_start, nodes_now, force_now):
        def one_rate(field_now):
            padded = jnp.pad(field_now, ((0, 0), (1, 1), (0, 0)))
            return rate_of(padded, decay_rate, mixing, diffusivity, velocity, force_now)

        node_rates = jax.vmap(one_rate)(nodes_now)
        summed = jnp.einsum("mj,jsxc->msxc", q_table, node_rates, precision=lax.Precision.HIGHEST)
        return (slice_start[None] + time_step * summed + stiff_part * nodes_now) / (1.0 + stiff_part)

    def slice_end(inputs_now):
        slice_start, force_now = inputs_now
        return sweep_nodes(slice_start, first_nodes(slice_start, force_now), force_now)[-1]

    ends = lax.map(slice_end, (starts, forcing))
    handed = jnp.concatenate([initial[None], ends[:-1]], axis=0)

    def slice_final(inputs_now):
        slice_start, second_start, force_now = inputs_now
        first_pass = sweep_nodes(slice_start, first_nodes(slice_start, force_now), force_now)
        return sweep_nodes(second_start, first_pass, force_now)

    return lax.map(slice_final, (starts, handed, forcing))
```

```python
import jax
import jax.numpy as jnp
import numpy as np
from jax import lax
from jax.sharding import PartitionSpec as P

NZ = 16
TEAM = 4
time_step = 0.05


def quadrature(node_count):
    points = [(position + 1.0) / node_count for position in range(node_count)]
    weights_table = np.zeros((node_count, node_count))
    for column in range(node_count):
        coeffs = [1.0]
        denominator = 1.0
        for other_node in range(node_count):
            if other_node != column:
                shifted = [0.0] + coeffs
                for degree in range(len(coeffs)):
                    shifted[degree] = shifted[degree] - points[other_node] * coeffs[degree]
                coeffs = shifted
                denominator = denominator * (points[column] - points[other_node])
        for row_node in range(node_count):
            running = 0.0
            for degree in range(len(coeffs)):
                running = running + coeffs[degree] * points[row_node] ** (degree + 1) / (degree + 1)
            weights_table[row_node, column] = running / denominator
    return (weights_table, np.array(points))


def rates(v, decay_rate, mixing, diffusivity, velocity, force):
    center = v[:, :, 1:-1]
    x_plus = v[:, :, 2:]
    x_minus = v[:, :, :-2]
    y_plus = jnp.roll(center, -NZ, axis=3)
    y_minus = jnp.roll(center, NZ, axis=3)
    depth = jnp.arange(center.shape[3]) % NZ
    z_plus = jnp.where(depth == NZ - 1, 0.0, jnp.roll(center, -1, axis=3))
    z_minus = jnp.where(depth == 0, 0.0, jnp.roll(center, 1, axis=3))
    laplace = x_plus + x_minus + (y_plus + y_minus) + (z_plus + z_minus) - 6.0 * center
    drift = (
        velocity[0][:, None, None] * (x_plus - x_minus)
        + velocity[1][:, None, None] * (y_plus - y_minus)
        + velocity[2][:, None, None] * (z_plus - z_minus)
    )
    species = mixing.shape[0]
    coupled = sum(mixing[:, t][:, None, None] * center[:, t][:, None] for t in range(species))
    return (
        diffusivity[:, None, None] * laplace
        - 0.5 * drift
        - decay_rate * center
        + jnp.tanh(coupled)
        + force
    )


def slice_starts(initial, force, decay_rate):
    slices = lax.axis_size("tm")
    place = lax.axis_index("tm")
    member = place % TEAM
    team = place // TEAM
    teams = slices // TEAM
    groups = [[TEAM * g + i for i in range(TEAM)] for g in range(teams)]
    factor = 1.0 / (1.0 + time_step * decay_rate)
    handover = lax.ppermute(force, "tm", [(TEAM * g - 1, TEAM * g) for g in range(1, teams)])
    gathered = lax.all_gather(force, "tm", axis_index_groups=groups)
    share = force.shape[0] // TEAM

    def own(array, axis):
        return lax.dynamic_slice_in_dim(array, member * share, share, axis)

    own_factor = own(factor, 0)
    own_gathered = own(gathered, 1)
    total = jnp.zeros_like(own_factor)
    for k in range(TEAM):
        total = own_factor * (total + time_step * own_gathered[k])
    factor2 = own_factor * own_factor
    factor4 = factor2 * factor2
    arrived = [
        lax.ppermute(total, "tm", [(p, p + TEAM * d) for p in range(slices - TEAM * d)])
        for d in range(1, teams)
    ]
    own_initial = own(initial, 0)
    state = jnp.zeros_like(own_factor)
    for d in range(teams - 1, 0, -1):
        state = jnp.where(team == d, own_initial, state)
        state = factor4 * state + arrived[d - 1]
    state = jnp.where(team == 0, own_initial, state)
    base = lax.all_gather(state, "tm", axis=0, tiled=True, axis_index_groups=groups)

    start = base
    before = base * (1.0 + time_step * decay_rate) - time_step * handover
    force_before = handover
    for k in range(TEAM - 1):
        passed = member > k
        before = jnp.where(passed, start, before)
        force_before = jnp.where(passed, gathered[k], force_before)
        start = jnp.where(passed, factor * (start + time_step * gathered[k]), start)
    return start, before, force_before


def body(initial, forcing, decay_rate, mixing, diffusivity, velocity):
    node_count = lax.axis_size("node")
    node_index = lax.axis_index("node")
    weights_table, points = quadrature(node_count)
    q_table = jnp.asarray(weights_table, jnp.float32)
    times = jnp.asarray(points, jnp.float32)[:, None, None, None]
    own_row = lax.dynamic_index_in_dim(q_table, node_index, 0, False)
    force = forcing[0]
    start, before, force_before = slice_starts(initial, force, decay_rate)

    tiles = lax.axis_size("space")
    tile = lax.axis_index("space")
    fields = jnp.stack([start, before, force, force_before, decay_rate])
    up = [(i, i + 1) for i in range(tiles - 1)]
    down = [(j, i) for i, j in up]
    below = lax.ppermute(fields[:, :, -2:], "space", up)
    above = lax.ppermute(fields[:, :, :2], "space", down)
    fields = jnp.concatenate([below, fields, above], axis=2)
    start_w, before_w, force_w, force_before_w, decay_w = [fields[k] for k in range(5)]

    def first_sweep(start_w, force_w, decay_w, rows):
        v0 = (start_w[None] + times * time_step * force_w[None]) / (
            1.0 + times * time_step * decay_w[None]
        )
        inner = decay_w[:, 1:-1]
        rate = rates(v0, inner, mixing, diffusivity, velocity, force_w[:, 1:-1])
        out = []
        for m in rows:
            summed = sum(float(np.float32(weights_table[m, j])) * rate[j] for j in range(node_count))
            stiff = float(np.float32(time_step * points[m] / node_count)) * inner
            out.append((start_w[:, 1:-1] + time_step * summed + stiff * v0[m][:, 1:-1]) / (1.0 + stiff))
        return jnp.stack(out)

    v1 = first_sweep(start_w, force_w, decay_w, range(node_count))
    planes = v1.shape[2]
    row = jnp.arange(planes)[:, None]
    outside = ((tile == 0) & (row == 0)) | ((tile == tiles - 1) & (row == planes - 1))
    v1 = jnp.where(outside, 0.0, v1)
    inner = slice(1, -1)
    handed = first_sweep(
        before_w[:, inner], force_before_w[:, inner], decay_w[:, inner], [node_count - 1]
    )[0]
    second_start = jnp.where(
        lax.axis_index("tm") == 0, initial, handed
    )
    rate = rates(v1, decay_rate, mixing, diffusivity, velocity, force)
    summed = jnp.sum(own_row[:, None, None, None] * rate, axis=0)
    own_v1 = lax.dynamic_index_in_dim(v1, node_index, 0, False)[:, inner]
    own_time = (node_index.astype(jnp.float32) + 1.0) / node_count
    stiff = time_step * (own_time / node_count) * decay_rate
    final = (second_start + time_step * summed + stiff * own_v1) / (1.0 + stiff)
    return final[None, None]


def solution(mesh):
    placed = (
        P(None, "space", None),
        P("tm", None, "space", None),
        P(None, "space", None),
        P(),
        P(),
        P(),
    )
    return jax.shard_map(
        body,
        mesh=mesh,
        in_specs=placed,
        out_specs=P("tm", "node", None, "space", None),
        check_vma=False,
    )
```

```python
import jax
import jax.numpy as jnp
import numpy as np
from jax import lax
from jax.experimental import pallas as pl
from jax.experimental.pallas import tpu as pltpu
from jax.sharding import PartitionSpec as P

NZ = 16
TEAM = 4
time_step = 0.05


def quadrature(node_count):
    points = [(position + 1.0) / node_count for position in range(node_count)]
    weights_table = np.zeros((node_count, node_count))
    for column in range(node_count):
        coeffs = [1.0]
        denominator = 1.0
        for other_node in range(node_count):
            if other_node != column:
                shifted = [0.0] + coeffs
                for degree in range(len(coeffs)):
                    shifted[degree] = shifted[degree] - points[other_node] * coeffs[degree]
                coeffs = shifted
                denominator = denominator * (points[column] - points[other_node])
        for row_node in range(node_count):
            running = 0.0
            for degree in range(len(coeffs)):
                running = running + coeffs[degree] * points[row_node] ** (degree + 1) / (degree + 1)
            weights_table[row_node, column] = running / denominator
    return (weights_table, np.array(points))


def total(terms):
    terms = list(terms)
    while len(terms) > 1:
        terms = [sum(terms[i : i + 2]) for i in range(0, len(terms), 2)]
    return terms[0]


def stencil(s, diff_ref, vel_ref, shape):
    rows, cells = shape
    d, vx, vy, vz = diff_ref[s], 0.5 * vel_ref[0, s], 0.5 * vel_ref[1, s], 0.5 * vel_ref[2, s]
    depth = lax.broadcasted_iota(jnp.int32, shape, 1) % NZ
    up = jnp.where(depth == NZ - 1, 0.0, d - vz)
    down = jnp.where(depth == 0, 0.0, d + vz)

    def apply(v, x_plus, x_minus, decay):
        y_plus = pltpu.roll(v, cells - NZ, 1)
        y_minus = pltpu.roll(v, NZ, 1)
        z_plus = pltpu.roll(v, cells - 1, 1)
        z_minus = pltpu.roll(v, 1, 1)
        return total(
            [
                (d - vx) * x_plus,
                (d + vx) * x_minus,
                (d - vy) * y_plus,
                (d + vy) * y_minus,
                up * z_plus,
                down * z_minus,
                (-6.0 * d - decay) * v,
            ]
        )

    return apply


def coupling(s, v_ref, j, mix_ref):
    return jnp.tanh(total(mix_ref[s, t] * v_ref[j, t] for t in range(v_ref.shape[1])))


def node_starts(s, points, start, force, decay, v_ref):
    for j, tau in enumerate(points):
        step = float(tau * time_step)
        v_ref[j, s] = (start + step * force) / (1.0 + step * decay)


def node_rates(s, v_ref, force, decay, mix_ref, apply):
    rows = v_ref.shape[2]
    out = []
    for j in range(v_ref.shape[0]):
        v = v_ref[j, s]
        moved = apply(v, pltpu.roll(v, rows - 1, 0), pltpu.roll(v, 1, 0), decay)
        out.append(moved + (coupling(s, v_ref, j, mix_ref) + force))
    return out


def swept(m, weights, points, rates, base, v, decay):
    count = len(rates)
    summed = total(float(time_step * weights[m, j]) * rates[j] for j in range(count))
    stiff = float(time_step * points[m] / count) * decay
    return (base + summed + stiff * v) / (1.0 + stiff)


def first_sweep(start_ref, before_ref, force_ref, force_before_ref, decay_ref, mix_ref, diff_ref,
                vel_ref, v_ref, w_ref, v1_ref, handed_ref):
    species, rows, cells = start_ref.shape
    count = v_ref.shape[0]
    weights, points = quadrature(count)

    def begin(s, carry):
        decay = decay_ref[s]
        node_starts(s, points, start_ref[s], force_ref[s], decay, v_ref)
        node_starts(s, points, before_ref[s], force_before_ref[s], decay, w_ref)
        return carry

    lax.fori_loop(0, species, begin, 0)

    def sweep(s, carry):
        decay = decay_ref[s]
        apply = stencil(s, diff_ref, vel_ref, (rows, cells))
        rates = node_rates(s, v_ref, force_ref[s], decay, mix_ref, apply)
        for m in range(count):
            v1_ref[m, s] = swept(m, weights, points, rates, start_ref[s], v_ref[m, s], decay)
        return carry

    lax.fori_loop(0, species, sweep, 0)

    def sweep_before(s, carry):
        decay = decay_ref[s]
        apply = stencil(s, diff_ref, vel_ref, (rows, cells))
        rates = node_rates(s, w_ref, force_before_ref[s], decay, mix_ref, apply)
        m = count - 1
        handed_ref[s] = swept(m, weights, points, rates, before_ref[s], w_ref[m, s], decay)
        return carry

    lax.fori_loop(0, species, sweep_before, 0)


def inner_kernel(start_ref, before_ref, force_ref, force_before_ref, decay_ref, mix_ref, diff_ref,
                 vel_ref, v1_ref, handed_ref, v_ref, w_ref):
    first_sweep(start_ref, before_ref, force_ref, force_before_ref, decay_ref, mix_ref, diff_ref,
                vel_ref, v_ref, w_ref, v1_ref, handed_ref)


def start_kernel(place_ref, base_ref, gathered_ref, handover_ref, force_ref, decay_ref, start_ref,
                 before_ref, force_before_ref, low_ref, high_ref):
    member = place_ref[0]
    planes = base_ref.shape[1]
    for s in range(base_ref.shape[0]):
        base, decay = base_ref[s], decay_ref[s]
        grow = 1.0 + time_step * decay
        factor = 1.0 / grow
        start = base
        force_before = handover_ref[s]
        before = base * grow - time_step * force_before
        for k in range(TEAM - 1):
            passed = member > k
            force = gathered_ref[k, s]
            before = jnp.where(passed, start, before)
            force_before = jnp.where(passed, force, force_before)
            start = jnp.where(passed, factor * (start + time_step * force), start)
        start_ref[s] = start
        before_ref[s] = before
        force_before_ref[s] = force_before
        for k, field in enumerate((start, before, force_ref[s], force_before, decay)):
            low_ref[k, s] = field[:2]
            high_ref[k, s] = field[planes - 2 :]


def outer_kernel(place_ref, row_ref, start_ref, before_ref, force_ref, force_before_ref, decay_ref,
                 initial_ref, below_ref, above_ref, v1_ref, handed_ref, mix_ref, diff_ref, vel_ref,
                 out_ref, e_ref, v_ref, w_ref, v1e_ref, handede_ref, full_ref):
    node, slot, tile, tiles = place_ref[1], place_ref[2], place_ref[3], place_ref[4]
    species, planes, cells = start_ref.shape
    count = v_ref.shape[0]
    for k, ref in enumerate((start_ref, before_ref, force_ref, force_before_ref, decay_ref)):
        for s in range(species):
            e_ref[k, s, 0:2] = below_ref[k, s]
            e_ref[k, s, 2:4] = ref[s, 0:2]
            e_ref[k, s, 4:6] = ref[s, planes - 2 : planes]
            e_ref[k, s, 6:8] = above_ref[k, s]
    first_sweep(e_ref.at[0], e_ref.at[1], e_ref.at[2], e_ref.at[3], e_ref.at[4], mix_ref, diff_ref,
                vel_ref, v_ref, w_ref, v1e_ref, handede_ref)
    edge = lax.broadcasted_iota(jnp.int32, (8, cells), 0)
    outside = ((tile == 0) & (edge == 1)) | ((tile == tiles - 1) & (edge == 6))
    row = lax.broadcasted_iota(jnp.int32, (planes, cells), 0)

    def fill(s, carry):
        for j in range(count):
            v1e = v1e_ref[j, s]
            v1e_ref[j, s] = jnp.where(outside, 0.0, v1e)
            full_ref[j, s] = v1_ref[j, s]
            full_ref[j, s, 0:1] = v1e[2:3]
            full_ref[j, s, planes - 1 : planes] = v1e[5:6]
        return carry

    lax.fori_loop(0, species, fill, 0)
    scale = float(time_step / count / count)
    stiff_of_node = scale * (node + 1).astype(jnp.float32)

    def finish(s, carry):
        decay = decay_ref[s]
        apply = stencil(s, diff_ref, vel_ref, (planes, cells))
        mixed = total(row_ref[j] * full_ref[j, s] for j in range(count))
        mixed_edge = total(row_ref[j] * v1e_ref[j, s] for j in range(count))
        x_plus = jnp.where(row == planes - 1, mixed_edge[6:7], pltpu.roll(mixed, planes - 1, 0))
        x_minus = jnp.where(row == 0, mixed_edge[1:2], pltpu.roll(mixed, 1, 0))
        coupled = total(row_ref[j] * coupling(s, full_ref, j, mix_ref) for j in range(count))
        weight = total(row_ref[j] for j in range(count))
        summed = apply(mixed, x_plus, x_minus, decay) + coupled + weight * force_ref[s]
        handede = handede_ref[s]
        handed = handed_ref[s]
        handed = jnp.where(row == 0, handede[2:3], handed)
        handed = jnp.where(row == planes - 1, handede[5:6], handed)
        second_start = jnp.where(slot == 0, initial_ref[s], handed)
        stiff = stiff_of_node * decay
        own = full_ref[node, s]
        out_ref[0, 0, s] = (second_start + time_step * summed + stiff * own) / (1.0 + stiff)
        return carry

    lax.fori_loop(0, species, finish, 0)


def call(kernel, outs, ins, scratch, cost):
    spaces = [pltpu.SMEM if kind == "s" else pltpu.VMEM for kind in ins]
    return pl.pallas_call(
        kernel,
        out_shape=[jax.ShapeDtypeStruct(shape, jnp.float32) for shape in outs],
        in_specs=[pl.BlockSpec(memory_space=space) for space in spaces],
        out_specs=[pl.BlockSpec(memory_space=pltpu.VMEM)] * len(outs),
        scratch_shapes=[pltpu.VMEM(shape, jnp.float32) for shape in scratch],
        cost_estimate=pl.CostEstimate(flops=cost, bytes_accessed=cost // 8, transcendentals=0),
        compiler_params=pltpu.CompilerParams(vmem_limit_bytes=24 * 2**20),
    )


def team_base(initial, force, decay_rate):
    slices = lax.axis_size("tm")
    place = lax.axis_index("tm")
    member = place % TEAM
    team = place // TEAM
    teams = slices // TEAM
    groups = [[TEAM * g + i for i in range(TEAM)] for g in range(teams)]
    handover = lax.ppermute(force, "tm", [(TEAM * g - 1, TEAM * g) for g in range(1, teams)])
    gathered = lax.all_gather(force, "tm", axis_index_groups=groups)
    share = force.shape[0] // TEAM

    def own(array, axis):
        return lax.dynamic_slice_in_dim(array, member * share, share, axis)

    factor = 1.0 / (1.0 + time_step * own(decay_rate, 0))
    own_gathered = own(gathered, 1)
    summed = jnp.zeros_like(factor)
    for k in range(TEAM):
        summed = factor * (summed + time_step * own_gathered[k])
    factor2 = factor * factor
    factor4 = factor2 * factor2

    def forward(value, distance, senders):
        pairs = [(TEAM * g + i, TEAM * (g + distance) + i) for g in senders for i in range(TEAM)]
        return lax.ppermute(value, "tm", pairs)

    near = forward(summed, 1, range(teams - 1))
    own_initial = own(initial, 0)
    state = jnp.where(team == 0, own_initial, factor4 * own_initial + near)
    for first in range(0, teams - 2, 2):
        senders = range(first, min(first + 2, teams - 2))
        ahead = forward(factor4 * state + summed, 2, senders)
        reached = (team == first + 2) | (team == first + 3)
        state = jnp.where(reached, factor4 * ahead + near, state)
    base = lax.all_gather(state, "tm", axis=0, tiled=True, axis_index_groups=groups)
    return base, gathered, handover


def body(initial, forcing, decay_rate, mixing, diffusivity, velocity):
    count = lax.axis_size("node")
    node = lax.axis_index("node")
    place = lax.axis_index("tm")
    tiles = lax.axis_size("space")
    tile = lax.axis_index("space")
    force = forcing[0]
    base, gathered, handover = team_base(initial, force, decay_rate)
    where_am_i = jnp.stack([place % TEAM, node, place, tile, jnp.int32(tiles)]).astype(jnp.int32)
    weights = jnp.asarray(quadrature(count)[0], jnp.float32)
    own_row = lax.dynamic_index_in_dim(weights, node, 0, False)

    full = force.shape
    species, planes, cells = full
    edge = (5, species, 2, cells)
    start, before, force_before, low, high = call(
        start_kernel, [full, full, full, edge, edge], "svvvvv", [], 2**20
    )(where_am_i, base, gathered, handover, force, decay_rate)
    up = [(i, i + 1) for i in range(tiles - 1)]
    down = [(j, i) for i, j in up]
    below = lax.ppermute(high, "space", up)
    above = lax.ppermute(low, "space", down)
    nodes = (count,) + full
    params = (mixing, diffusivity, velocity)
    fields = (start, before, force, force_before, decay_rate)
    v1, handed = call(inner_kernel, [nodes, full], "vvvvvsss", [nodes, nodes], 2**25)(
        *fields, *params
    )
    small = (species, 8, cells)
    edges = (count,) + small
    (out,) = call(
        outer_kernel,
        [(1, 1) + full],
        "ss" + "v" * 10 + "sss",
        [(5,) + small, edges, edges, edges, small, nodes],
        2**25,
    )(where_am_i, own_row, *fields, initial, below, above, v1, handed, *params)
    return out


def solution(mesh):
    placed = (
        P(None, "space", None),
        P("tm", None, "space", None),
        P(None, "space", None),
        P(),
        P(),
        P(),
    )
    return jax.shard_map(
        body,
        mesh=mesh,
        in_specs=placed,
        out_specs=P("tm", "node", None, "space", None),
        check_vma=False,
    )
```

```python
import jax
import jax.numpy as jnp
import numpy as np
from jax import lax
from jax.experimental import pallas as pl
from jax.experimental.pallas import tpu as pltpu
from jax.sharding import PartitionSpec as P

NZ = 16
TEAM = 4
time_step = 0.05


def quadrature(node_count):
    points = [(position + 1.0) / node_count for position in range(node_count)]
    weights_table = np.zeros((node_count, node_count))
    for column in range(node_count):
        coeffs = [1.0]
        denominator = 1.0
        for other_node in range(node_count):
            if other_node != column:
                shifted = [0.0] + coeffs
                for degree in range(len(coeffs)):
                    shifted[degree] = shifted[degree] - points[other_node] * coeffs[degree]
                coeffs = shifted
                denominator = denominator * (points[column] - points[other_node])
        for row_node in range(node_count):
            running = 0.0
            for degree in range(len(coeffs)):
                running = running + coeffs[degree] * points[row_node] ** (degree + 1) / (degree + 1)
            weights_table[row_node, column] = running / denominator
    return (weights_table, np.array(points))


def total(terms):
    out = None
    for term in terms:
        out = term if out is None else out + term
    return out


def stencil(s, diff_ref, vel_ref, shape):
    rows, cells = shape
    d, vx, vy, vz = diff_ref[s], 0.5 * vel_ref[0, s], 0.5 * vel_ref[1, s], 0.5 * vel_ref[2, s]
    depth = lax.broadcasted_iota(jnp.int32, shape, 1) % NZ
    up = jnp.where(depth == NZ - 1, 0.0, d - vz)
    down = jnp.where(depth == 0, 0.0, d + vz)

    def apply(v, x_plus, x_minus, decay):
        y_plus = pltpu.roll(v, cells - NZ, 1)
        y_minus = pltpu.roll(v, NZ, 1)
        z_plus = pltpu.roll(v, cells - 1, 1)
        z_minus = pltpu.roll(v, 1, 1)
        return total(
            [
                (d - vx) * x_plus,
                (d + vx) * x_minus,
                (d - vy) * y_plus,
                (d + vy) * y_minus,
                up * z_plus,
                down * z_minus,
                (-6.0 * d - decay) * v,
            ]
        )

    return apply


def coupling(s, v_ref, j, mix_ref):
    return jnp.tanh(total(mix_ref[s, t] * v_ref[j, t] for t in range(v_ref.shape[1])))


def node_starts(s, points, fields, decay):
    for j, tau in enumerate(points):
        step = float(tau * time_step)
        shrink = 1.0 / (1.0 + step * decay)
        for start, force, v_ref in fields:
            v_ref[j, s] = (start + step * force) * shrink


def node_rates(s, v_ref, force, decay, mix_ref, apply):
    rows = v_ref.shape[2]
    out = []
    for j in range(v_ref.shape[0]):
        v = v_ref[j, s]
        moved = apply(v, pltpu.roll(v, rows - 1, 0), pltpu.roll(v, 1, 0), decay)
        out.append(moved + (coupling(s, v_ref, j, mix_ref) + force))
    return out


def swept(m, weights, points, rates, base, v, decay):
    count = len(rates)
    summed = total(float(time_step * weights[m, j]) * rates[j] for j in range(count))
    stiff = float(time_step * points[m] / count) * decay
    return (base + summed + stiff * v) / (1.0 + stiff)


def first_sweep(start_ref, before_ref, force_ref, force_before_ref, decay_ref, mix_ref, diff_ref,
                vel_ref, v_ref, w_ref, v1_ref, handed_ref, ready):
    species, rows, cells = start_ref.shape
    count = v_ref.shape[0]
    weights, points = quadrature(count)

    def begin(s, carry):
        decay = decay_ref[s]
        now = (start_ref[s], force_ref[s], v_ref)
        then = (before_ref[s], force_before_ref[s], w_ref)
        node_starts(s, points, (now, then), decay)
        return carry

    lax.fori_loop(0, species, begin, 0, unroll=4)

    ready()

    def sweep(s, carry):
        decay = decay_ref[s]
        apply = stencil(s, diff_ref, vel_ref, (rows, cells))
        rates = node_rates(s, v_ref, force_ref[s], decay, mix_ref, apply)
        for m in range(count):
            v1_ref[m, s] = swept(m, weights, points, rates, start_ref[s], v_ref[m, s], decay)
        return carry

    lax.fori_loop(0, species, sweep, 0, unroll=4)

    def sweep_before(s, carry):
        decay = decay_ref[s]
        apply = stencil(s, diff_ref, vel_ref, (rows, cells))
        m = count - 1
        row = [float(time_step * weights[m, j]) for j in range(count)]
        mixed = total(row[j] * w_ref[j, s] for j in range(count))
        coupled = total(row[j] * coupling(s, w_ref, j, mix_ref) for j in range(count))
        moved = apply(mixed, pltpu.roll(mixed, rows - 1, 0), pltpu.roll(mixed, 1, 0), decay)
        stiff = float(time_step * points[m] / count) * decay
        base = before_ref[s] + float(sum(row)) * force_before_ref[s]
        handed_ref[s] = (base + (moved + coupled) + stiff * w_ref[m, s]) / (1.0 + stiff)
        return carry

    lax.fori_loop(0, species, sweep_before, 0, unroll=4)


def fetch(sources, targets, sems):
    copies = [pltpu.make_async_copy(a, b, sems.at[i]) for i, (a, b) in enumerate(zip(sources, targets))]
    for copy in copies:
        copy.start()

    def ready():
        for copy in copies:
            copy.wait()

    return ready


def inner_kernel(start_ref, before_ref, force_ref, force_before_ref, decay_ref, mix_hbm, diff_hbm,
                 vel_hbm, v1_ref, handed_ref, v_ref, w_ref, mix_ref, diff_ref, vel_ref, sems):
    ready = fetch((mix_hbm, diff_hbm, vel_hbm), (mix_ref, diff_ref, vel_ref), sems)
    first_sweep(start_ref, before_ref, force_ref, force_before_ref, decay_ref, mix_ref, diff_ref,
                vel_ref, v_ref, w_ref, v1_ref, handed_ref, ready)


def start_kernel(place_ref, base_ref, gathered_ref, handover_ref, force_ref, decay_ref, start_ref,
                 before_ref, force_before_ref, low_ref, high_ref):
    member = place_ref[0]
    planes = base_ref.shape[1]
    for s in range(base_ref.shape[0]):
        base, decay = base_ref[s], decay_ref[s]
        grow = 1.0 + time_step * decay
        factor = 1.0 / grow
        start = base
        force_before = handover_ref[s]
        before = base * grow - time_step * force_before
        for k in range(TEAM - 1):
            passed = member > k
            force = gathered_ref[k, s]
            before = jnp.where(passed, start, before)
            force_before = jnp.where(passed, force, force_before)
            start = jnp.where(passed, factor * (start + time_step * force), start)
        start_ref[s] = start
        before_ref[s] = before
        force_before_ref[s] = force_before
        for k, field in enumerate((start, before, force_ref[s], force_before, decay)):
            low_ref[k, s] = field[:2]
            high_ref[k, s] = field[planes - 2 :]


def outer_kernel(place_ref, start_ref, before_ref, force_ref, force_before_ref, decay_ref,
                 initial_ref, below_ref, above_ref, v1_ref, handed_ref, mix_hbm, diff_hbm, vel_hbm,
                 out_ref, e_ref, v_ref, w_ref, v1e_ref, handede_ref, full_ref, mix_ref, diff_ref,
                 vel_ref, sems):
    ready = fetch((mix_hbm, diff_hbm, vel_hbm), (mix_ref, diff_ref, vel_ref), sems)
    node, slot, tile, tiles = place_ref[1], place_ref[2], place_ref[3], place_ref[4]
    species, planes, cells = start_ref.shape
    count = v_ref.shape[0]
    for k, ref in enumerate((start_ref, before_ref, force_ref, force_before_ref, decay_ref)):
        for s in range(species):
            e_ref[k, s, 0:2] = below_ref[k, s]
            e_ref[k, s, 2:4] = ref[s, 0:2]
            e_ref[k, s, 4:6] = ref[s, planes - 2 : planes]
            e_ref[k, s, 6:8] = above_ref[k, s]
    first_sweep(e_ref.at[0], e_ref.at[1], e_ref.at[2], e_ref.at[3], e_ref.at[4], mix_ref, diff_ref,
                vel_ref, v_ref, w_ref, v1e_ref, handede_ref, ready)
    edge = lax.broadcasted_iota(jnp.int32, (8, cells), 0)
    outside = ((tile == 0) & (edge == 1)) | ((tile == tiles - 1) & (edge == 6))
    row = lax.broadcasted_iota(jnp.int32, (planes, cells), 0)

    def fill(s, carry):
        for j in range(count):
            v1e = v1e_ref[j, s]
            v1e_ref[j, s] = jnp.where(outside, 0.0, v1e)
            full_ref[j, s] = v1_ref[j, s]
            full_ref[j, s, 0:1] = v1e[2:3]
            full_ref[j, s, planes - 1 : planes] = v1e[5:6]
        return carry

    lax.fori_loop(0, species, fill, 0, unroll=4)
    weights = quadrature(count)[0]
    own_row = []
    for j in range(count):
        weight = jnp.float32(weights[0, j])
        for m in range(1, count):
            weight = jnp.where(node == m, jnp.float32(weights[m, j]), weight)
        own_row.append(weight)
    scale = float(time_step / count / count)
    stiff_of_node = scale * (node + 1).astype(jnp.float32)

    def finish(s, carry):
        decay = decay_ref[s]
        apply = stencil(s, diff_ref, vel_ref, (planes, cells))
        mixed = total(own_row[j] * full_ref[j, s] for j in range(count))
        mixed_edge = total(own_row[j] * v1e_ref[j, s] for j in range(count))
        x_plus = jnp.where(row == planes - 1, mixed_edge[6:7], pltpu.roll(mixed, planes - 1, 0))
        x_minus = jnp.where(row == 0, mixed_edge[1:2], pltpu.roll(mixed, 1, 0))
        coupled = total(own_row[j] * coupling(s, full_ref, j, mix_ref) for j in range(count))
        weight = total(own_row[j] for j in range(count))
        summed = apply(mixed, x_plus, x_minus, decay) + coupled + weight * force_ref[s]
        handede = handede_ref[s]
        handed = handed_ref[s]
        handed = jnp.where(row == 0, handede[2:3], handed)
        handed = jnp.where(row == planes - 1, handede[5:6], handed)
        second_start = jnp.where(slot == 0, initial_ref[s], handed)
        stiff = stiff_of_node * decay
        own = full_ref[node, s]
        out_ref[0, 0, s] = (second_start + time_step * summed + stiff * own) / (1.0 + stiff)
        return carry

    lax.fori_loop(0, species, finish, 0, unroll=4)


def call(kernel, outs, ins, scratch, cost, params=()):
    spaces = [{"s": pltpu.SMEM, "v": pltpu.VMEM, "h": pltpu.HBM}[kind] for kind in ins]
    scratch = [pltpu.VMEM(shape, jnp.float32) for shape in scratch]
    if "h" in ins:
        scratch += [pltpu.SMEM(shape, jnp.float32) for shape in params]
        scratch += [pltpu.SemaphoreType.DMA((len(params),))]
    return pl.pallas_call(
        kernel,
        out_shape=[jax.ShapeDtypeStruct(shape, jnp.float32) for shape in outs],
        in_specs=[pl.BlockSpec(memory_space=space) for space in spaces],
        out_specs=[pl.BlockSpec(memory_space=pltpu.VMEM)] * len(outs),
        scratch_shapes=scratch,
        cost_estimate=pl.CostEstimate(flops=cost, bytes_accessed=cost // 8, transcendentals=0),
        compiler_params=pltpu.CompilerParams(vmem_limit_bytes=24 * 2**20),
    )


def team_base(initial, force, decay_rate):
    slices = lax.axis_size("tm")
    place = lax.axis_index("tm")
    member = place % TEAM
    team = place // TEAM
    teams = slices // TEAM
    groups = [[TEAM * g + i for i in range(TEAM)] for g in range(teams)]
    handover = lax.ppermute(force, "tm", [(TEAM * g - 1, TEAM * g) for g in range(1, teams)])
    gathered = lax.all_gather(force, "tm", axis_index_groups=groups)
    share = force.shape[0] // TEAM

    def own(array, axis):
        return lax.dynamic_slice_in_dim(array, member * share, share, axis)

    factor = 1.0 / (1.0 + time_step * own(decay_rate, 0))
    own_gathered = own(gathered, 1)
    summed = jnp.zeros_like(factor)
    for k in range(TEAM):
        summed = factor * (summed + time_step * own_gathered[k])
    factor2 = factor * factor
    factor4 = factor2 * factor2

    def send(value, *routes):
        pairs = [(TEAM * g + i, TEAM * t + i) for g, t in routes for i in range(TEAM)]
        return lax.ppermute(value, "tm", pairs)

    middle = teams // 2 - 1
    near = send(summed, *((g, g + 1) for g in range(middle + 1, teams - 1, 2)))
    state = own(initial, 0)
    for g in range(middle):
        arrived = send(factor4 * state + summed, (g, g + 1))
        state = jnp.where(team == g + 1, arrived, state)
    waiting = []
    for g in range(middle, teams, 2):
        routes = waiting + ([(g, g + 2)] if g + 2 < teams else [])
        if routes:
            arrived = send(factor4 * state + summed, *routes)
            for _, t in waiting:
                state = jnp.where(team == t, arrived, state)
            state = jnp.where(team == g + 2, factor4 * arrived + near, state)
        waiting = [(g, g + 1)] if g + 1 < teams else []
    base = lax.all_gather(state, "tm", axis=0, tiled=True, axis_index_groups=groups)
    return base, gathered, handover


def body(initial, forcing, decay_rate, mixing, diffusivity, velocity):
    count = lax.axis_size("node")
    node = lax.axis_index("node")
    place = lax.axis_index("tm")
    tiles = lax.axis_size("space")
    tile = lax.axis_index("space")
    force = forcing[0]
    base, gathered, handover = team_base(initial, force, decay_rate)
    where_am_i = jnp.stack([place % TEAM, node, place, tile, jnp.int32(tiles)]).astype(jnp.int32)
    full = force.shape
    species, planes, cells = full
    edge = (5, species, 2, cells)
    start, before, force_before, low, high = call(
        start_kernel, [full, full, full, edge, edge], "svvvvv", [], 2**20
    )(where_am_i, base, gathered, handover, force, decay_rate)
    up = [(i, i + 1) for i in range(tiles - 1)]
    down = [(j, i) for i, j in up]
    below = lax.ppermute(high, "space", up)
    above = lax.ppermute(low, "space", down)
    nodes = (count,) + full
    params = (mixing, diffusivity, velocity)
    shapes = [param.shape for param in params]
    fields = (start, before, force, force_before, decay_rate)
    v1, handed = call(inner_kernel, [nodes, full], "vvvvvhhh", [nodes, nodes], 2**25, shapes)(
        *fields, *params
    )
    small = (species, 8, cells)
    edges = (count,) + small
    (out,) = call(
        outer_kernel,
        [(1, 1) + full],
        "s" + "v" * 10 + "hhh",
        [(5,) + small, edges, edges, edges, small, nodes],
        2**25,
        shapes,
    )(where_am_i, *fields, initial, below, above, v1, handed, *params)
    return out


def solution(mesh):
    placed = (
        P(None, "space", None),
        P("tm", None, "space", None),
        P(None, "space", None),
        P(),
        P(),
        P(),
    )
    return jax.shard_map(
        body,
        mesh=mesh,
        in_specs=placed,
        out_specs=P("tm", "node", None, "space", None),
        check_vma=False,
    )
```

```python
import jax
import jax.numpy as jnp
import numpy as np
from jax import lax
from jax.experimental import pallas as pl
from jax.experimental.pallas import tpu as pltpu
from jax.sharding import PartitionSpec as P

NZ = 16
TEAM = 4
time_step = 0.05


def quadrature(node_count):
    points = [(position + 1.0) / node_count for position in range(node_count)]
    weights_table = np.zeros((node_count, node_count))
    for column in range(node_count):
        coeffs = [1.0]
        denominator = 1.0
        for other_node in range(node_count):
            if other_node != column:
                shifted = [0.0] + coeffs
                for degree in range(len(coeffs)):
                    shifted[degree] = shifted[degree] - points[other_node] * coeffs[degree]
                coeffs = shifted
                denominator = denominator * (points[column] - points[other_node])
        for row_node in range(node_count):
            running = 0.0
            for degree in range(len(coeffs)):
                running = running + coeffs[degree] * points[row_node] ** (degree + 1) / (degree + 1)
            weights_table[row_node, column] = running / denominator
    return (weights_table, np.array(points))


def total(terms):
    out = None
    for term in terms:
        out = term if out is None else out + term
    return out


def stencil(s, diff_ref, vel_ref, shape):
    rows, cells = shape
    d, vx, vy, vz = diff_ref[s], 0.5 * vel_ref[0, s], 0.5 * vel_ref[1, s], 0.5 * vel_ref[2, s]
    depth = lax.broadcasted_iota(jnp.int32, shape, 1) % NZ
    up = jnp.where(depth == NZ - 1, 0.0, d - vz)
    down = jnp.where(depth == 0, 0.0, d + vz)

    def apply(v, x_plus, x_minus, decay):
        y_plus = pltpu.roll(v, cells - NZ, 1)
        y_minus = pltpu.roll(v, NZ, 1)
        z_plus = pltpu.roll(v, cells - 1, 1)
        z_minus = pltpu.roll(v, 1, 1)
        return total(
            [
                (d - vx) * x_plus,
                (d + vx) * x_minus,
                (d - vy) * y_plus,
                (d + vy) * y_minus,
                up * z_plus,
                down * z_minus,
                (-6.0 * d - decay) * v,
            ]
        )

    return apply


def coupling(s, v_ref, j, mix_ref):
    return jnp.tanh(total(mix_ref[s, t] * v_ref[j, t] for t in range(v_ref.shape[1])))


def node_starts(s, points, fields, decay):
    for j, tau in enumerate(points):
        step = float(tau * time_step)
        shrink = 1.0 / (1.0 + step * decay)
        for start, force, v_ref in fields:
            v_ref[j, s] = (start + step * force) * shrink


def node_rates(s, v_ref, force, decay, mix_ref, apply):
    rows = v_ref.shape[2]
    out = []
    for j in range(v_ref.shape[0]):
        v = v_ref[j, s]
        moved = apply(v, pltpu.roll(v, rows - 1, 0), pltpu.roll(v, 1, 0), decay)
        out.append(moved + (coupling(s, v_ref, j, mix_ref) + force))
    return out


def swept(m, weights, points, rates, base, v, decay):
    count = len(rates)
    summed = total(float(time_step * weights[m, j]) * rates[j] for j in range(count))
    stiff = float(time_step * points[m] / count) * decay
    return (base + summed + stiff * v) / (1.0 + stiff)


def first_sweep(start_ref, before_ref, force_ref, force_before_ref, decay_ref, mix_ref, diff_ref,
                vel_ref, v_ref, w_ref, v1_ref, handed_ref, ready):
    species, rows, cells = start_ref.shape
    count = v_ref.shape[0]
    weights, points = quadrature(count)

    def begin(s, carry):
        decay = decay_ref[s]
        now = (start_ref[s], force_ref[s], v_ref)
        then = (before_ref[s], force_before_ref[s], w_ref)
        node_starts(s, points, (now, then), decay)
        return carry

    lax.fori_loop(0, species, begin, 0, unroll=4)

    ready()

    def sweep(s, carry):
        decay = decay_ref[s]
        apply = stencil(s, diff_ref, vel_ref, (rows, cells))
        rates = node_rates(s, v_ref, force_ref[s], decay, mix_ref, apply)
        for m in range(count):
            v1_ref[m, s] = swept(m, weights, points, rates, start_ref[s], v_ref[m, s], decay)
        return carry

    lax.fori_loop(0, species, sweep, 0, unroll=4)

    def sweep_before(s, carry):
        decay = decay_ref[s]
        apply = stencil(s, diff_ref, vel_ref, (rows, cells))
        m = count - 1
        row = [float(time_step * weights[m, j]) for j in range(count)]
        mixed = total(row[j] * w_ref[j, s] for j in range(count))
        coupled = total(row[j] * coupling(s, w_ref, j, mix_ref) for j in range(count))
        moved = apply(mixed, pltpu.roll(mixed, rows - 1, 0), pltpu.roll(mixed, 1, 0), decay)
        stiff = float(time_step * points[m] / count) * decay
        base = before_ref[s] + float(sum(row)) * force_before_ref[s]
        handed_ref[s] = (base + (moved + coupled) + stiff * w_ref[m, s]) / (1.0 + stiff)
        return carry

    lax.fori_loop(0, species, sweep_before, 0, unroll=4)


def fetch(sources, targets, sems):
    copies = [pltpu.make_async_copy(a, b, sems.at[i]) for i, (a, b) in enumerate(zip(sources, targets))]
    for copy in copies:
        copy.start()

    def ready():
        for copy in copies:
            copy.wait()

    return ready


def inner_kernel(start_ref, before_ref, force_ref, force_before_ref, decay_ref, mix_hbm, diff_hbm,
                 vel_hbm, v1_ref, handed_ref, v_ref, w_ref, mix_ref, diff_ref, vel_ref, sems):
    ready = fetch((mix_hbm, diff_hbm, vel_hbm), (mix_ref, diff_ref, vel_ref), sems)
    first_sweep(start_ref, before_ref, force_ref, force_before_ref, decay_ref, mix_ref, diff_ref,
                vel_ref, v_ref, w_ref, v1_ref, handed_ref, ready)


def start_kernel(place_ref, base_ref, gathered_ref, handover_ref, force_ref, decay_ref, mix_hbm, diff_hbm,
                 vel_hbm, start_ref, before_ref, force_before_ref, low_ref, high_ref):
    del mix_hbm, diff_hbm, vel_hbm
    member = place_ref[0]
    planes = base_ref.shape[1]
    for s in range(base_ref.shape[0]):
        base, decay = base_ref[s], decay_ref[s]
        grow = 1.0 + time_step * decay
        factor = 1.0 / grow
        start = base
        force_before = handover_ref[s]
        before = base * grow - time_step * force_before
        for k in range(TEAM - 1):
            passed = member > k
            force = gathered_ref[k, s]
            before = jnp.where(passed, start, before)
            force_before = jnp.where(passed, force, force_before)
            start = jnp.where(passed, factor * (start + time_step * force), start)
        start_ref[s] = start
        before_ref[s] = before
        force_before_ref[s] = force_before
        for k, field in enumerate((start, before, force_ref[s], force_before, decay)):
            low_ref[k, s] = field[:2]
            high_ref[k, s] = field[planes - 2 :]


def outer_kernel(place_ref, start_ref, before_ref, force_ref, force_before_ref, decay_ref,
                 initial_ref, below_ref, above_ref, v1_ref, handed_ref, mix_hbm, diff_hbm, vel_hbm,
                 out_ref, e_ref, v_ref, w_ref, v1e_ref, handede_ref, full_ref, mix_ref, diff_ref,
                 vel_ref, sems):
    ready = fetch((mix_hbm, diff_hbm, vel_hbm), (mix_ref, diff_ref, vel_ref), sems)
    node, slot, tile, tiles = place_ref[1], place_ref[2], place_ref[3], place_ref[4]
    species, planes, cells = start_ref.shape
    count = v_ref.shape[0]
    for k, ref in enumerate((start_ref, before_ref, force_ref, force_before_ref, decay_ref)):
        for s in range(species):
            e_ref[k, s, 0:2] = below_ref[k, s]
            e_ref[k, s, 2:4] = ref[s, 0:2]
            e_ref[k, s, 4:6] = ref[s, planes - 2 : planes]
            e_ref[k, s, 6:8] = above_ref[k, s]
    first_sweep(e_ref.at[0], e_ref.at[1], e_ref.at[2], e_ref.at[3], e_ref.at[4], mix_ref, diff_ref,
                vel_ref, v_ref, w_ref, v1e_ref, handede_ref, ready)
    edge = lax.broadcasted_iota(jnp.int32, (8, cells), 0)
    outside = ((tile == 0) & (edge == 1)) | ((tile == tiles - 1) & (edge == 6))
    row = lax.broadcasted_iota(jnp.int32, (planes, cells), 0)

    def fill(s, carry):
        for j in range(count):
            v1e = v1e_ref[j, s]
            v1e_ref[j, s] = jnp.where(outside, 0.0, v1e)
            full_ref[j, s] = v1_ref[j, s]
            full_ref[j, s, 0:1] = v1e[2:3]
            full_ref[j, s, planes - 1 : planes] = v1e[5:6]
        return carry

    lax.fori_loop(0, species, fill, 0, unroll=4)
    weights = quadrature(count)[0]
    own_row = []
    for j in range(count):
        weight = jnp.float32(weights[0, j])
        for m in range(1, count):
            weight = jnp.where(node == m, jnp.float32(weights[m, j]), weight)
        own_row.append(weight)
    scale = float(time_step / count / count)
    stiff_of_node = scale * (node + 1).astype(jnp.float32)

    def finish(s, carry):
        decay = decay_ref[s]
        apply = stencil(s, diff_ref, vel_ref, (planes, cells))
        mixed = total(own_row[j] * full_ref[j, s] for j in range(count))
        mixed_edge = total(own_row[j] * v1e_ref[j, s] for j in range(count))
        x_plus = jnp.where(row == planes - 1, mixed_edge[6:7], pltpu.roll(mixed, planes - 1, 0))
        x_minus = jnp.where(row == 0, mixed_edge[1:2], pltpu.roll(mixed, 1, 0))
        coupled = total(own_row[j] * coupling(s, full_ref, j, mix_ref) for j in range(count))
        weight = total(own_row[j] for j in range(count))
        summed = apply(mixed, x_plus, x_minus, decay) + coupled + weight * force_ref[s]
        handede = handede_ref[s]
        handed = handed_ref[s]
        handed = jnp.where(row == 0, handede[2:3], handed)
        handed = jnp.where(row == planes - 1, handede[5:6], handed)
        second_start = jnp.where(slot == 0, initial_ref[s], handed)
        stiff = stiff_of_node * decay
        own = full_ref[node, s]
        out_ref[0, 0, s] = (second_start + time_step * summed + stiff * own) / (1.0 + stiff)
        return carry

    lax.fori_loop(0, species, finish, 0, unroll=4)


def call(kernel, outs, ins, scratch, cost, params=()):
    spaces = [{"s": pltpu.SMEM, "v": pltpu.VMEM, "h": pltpu.HBM}[kind] for kind in ins]
    scratch = [pltpu.VMEM(shape, jnp.float32) for shape in scratch]
    if params:
        scratch += [pltpu.SMEM(shape, jnp.float32) for shape in params]
        scratch += [pltpu.SemaphoreType.DMA((len(params),))]
    return pl.pallas_call(
        kernel,
        out_shape=[jax.ShapeDtypeStruct(shape, jnp.float32) for shape in outs],
        in_specs=[pl.BlockSpec(memory_space=space) for space in spaces],
        out_specs=[pl.BlockSpec(memory_space=pltpu.VMEM)] * len(outs),
        scratch_shapes=scratch,
        cost_estimate=pl.CostEstimate(flops=cost, bytes_accessed=cost // 8, transcendentals=0),
        compiler_params=pltpu.CompilerParams(vmem_limit_bytes=24 * 2**20),
    )


def team_base(initial, force, decay_rate):
    slices = lax.axis_size("tm")
    place = lax.axis_index("tm")
    member = place % TEAM
    team = place // TEAM
    teams = slices // TEAM
    groups = [[TEAM * g + i for i in range(TEAM)] for g in range(teams)]
    handover = lax.ppermute(force, "tm", [(TEAM * g - 1, TEAM * g) for g in range(1, teams)])
    gathered = lax.all_gather(force, "tm", axis_index_groups=groups)
    share = force.shape[0] // TEAM

    def own(array, axis):
        return lax.dynamic_slice_in_dim(array, member * share, share, axis)

    factor = 1.0 / (1.0 + time_step * own(decay_rate, 0))
    own_gathered = own(gathered, 1)
    summed = jnp.zeros_like(factor)
    for k in range(TEAM):
        summed = factor * (summed + time_step * own_gathered[k])
    factor2 = factor * factor
    factor4 = factor2 * factor2

    def send(value, *routes):
        pairs = [(TEAM * g + i, TEAM * t + i) for g, t in routes for i in range(TEAM)]
        return lax.ppermute(value, "tm", pairs)

    middle = teams // 2 - 1
    near = send(summed, *((g, g + 1) for g in range(middle + 1, teams - 1, 2)))
    state = own(initial, 0)
    for g in range(middle):
        arrived = send(factor4 * state + summed, (g, g + 1))
        state = jnp.where(team == g + 1, arrived, state)
    anchor = 0.0 * handover[0, :1, :1]
    beside = []
    for g in range(middle, teams - 1, 2):
        ahead = factor4 * state + summed + anchor
        if g + 2 < teams:
            arrived = send(ahead, (g, g + 2))
            state = jnp.where(team == g + 2, factor4 * arrived + near, state)
        beside.append((g + 1, send(ahead, (g, g + 1))))
    for t, arrived in beside:
        state = jnp.where(team == t, arrived, state)
    base = lax.all_gather(state, "tm", axis=0, tiled=True, axis_index_groups=groups)
    return base, gathered, handover


def body(initial, forcing, decay_rate, mixing, diffusivity, velocity):
    count = lax.axis_size("node")
    node = lax.axis_index("node")
    place = lax.axis_index("tm")
    tiles = lax.axis_size("space")
    tile = lax.axis_index("space")
    force = forcing[0]
    base, gathered, handover = team_base(initial, force, decay_rate)
    where_am_i = jnp.stack([place % TEAM, node, place, tile, jnp.int32(tiles)]).astype(jnp.int32)
    full = force.shape
    params = (mixing, diffusivity, velocity)
    species, planes, cells = full
    edge = (5, species, 2, cells)
    start, before, force_before, low, high = call(
        start_kernel, [full, full, full, edge, edge], "svvvvvhhh", [], 2**20
    )(where_am_i, base, gathered, handover, force, decay_rate, *params)
    up = [(i, i + 1) for i in range(tiles - 1)]
    down = [(j, i) for i, j in up]
    below = lax.ppermute(high, "space", up)
    above = lax.ppermute(low, "space", down)
    nodes = (count,) + full
    shapes = [param.shape for param in params]
    fields = (start, before, force, force_before, decay_rate)
    v1, handed = call(inner_kernel, [nodes, full], "vvvvvhhh", [nodes, nodes], 2**25, shapes)(
        *fields, *params
    )
    small = (species, 8, cells)
    edges = (count,) + small
    (out,) = call(
        outer_kernel,
        [(1, 1) + full],
        "s" + "v" * 10 + "hhh",
        [(5,) + small, edges, edges, edges, small, nodes],
        2**25,
        shapes,
    )(where_am_i, *fields, initial, below, above, v1, handed, *params)
    return out


def solution(mesh):
    placed = (
        P(None, "space", None),
        P("tm", None, "space", None),
        P(None, "space", None),
        P(),
        P(),
        P(),
    )
    return jax.shard_map(
        body,
        mesh=mesh,
        in_specs=placed,
        out_specs=P("tm", "node", None, "space", None),
        check_vma=False,
    )
```

```python
import jax
import jax.numpy as jnp
import numpy as np
from jax import lax
from jax.experimental import pallas as pl
from jax.experimental.pallas import tpu as pltpu
from jax.sharding import PartitionSpec as P

NZ = 16
TEAM = 4
time_step = 0.05


def quadrature(node_count):
    points = [(position + 1.0) / node_count for position in range(node_count)]
    weights_table = np.zeros((node_count, node_count))
    for column in range(node_count):
        coeffs = [1.0]
        denominator = 1.0
        for other_node in range(node_count):
            if other_node != column:
                shifted = [0.0] + coeffs
                for degree in range(len(coeffs)):
                    shifted[degree] = shifted[degree] - points[other_node] * coeffs[degree]
                coeffs = shifted
                denominator = denominator * (points[column] - points[other_node])
        for row_node in range(node_count):
            running = 0.0
            for degree in range(len(coeffs)):
                running = running + coeffs[degree] * points[row_node] ** (degree + 1) / (degree + 1)
            weights_table[row_node, column] = running / denominator
    return (weights_table, np.array(points))


def total(terms):
    out = None
    for term in terms:
        out = term if out is None else out + term
    return out


def stencil(s, diff_ref, vel_ref, shape):
    rows, cells = shape
    d, vx, vy, vz = diff_ref[s], 0.5 * vel_ref[0, s], 0.5 * vel_ref[1, s], 0.5 * vel_ref[2, s]
    depth = lax.broadcasted_iota(jnp.int32, shape, 1) % NZ
    up = jnp.where(depth == NZ - 1, 0.0, d - vz)
    down = jnp.where(depth == 0, 0.0, d + vz)

    def apply(v, x_plus, x_minus, decay):
        y_plus = pltpu.roll(v, cells - NZ, 1)
        y_minus = pltpu.roll(v, NZ, 1)
        z_plus = pltpu.roll(v, cells - 1, 1)
        z_minus = pltpu.roll(v, 1, 1)
        return total(
            [
                (d - vx) * x_plus,
                (d + vx) * x_minus,
                (d - vy) * y_plus,
                (d + vy) * y_minus,
                up * z_plus,
                down * z_minus,
                (-6.0 * d - decay) * v,
            ]
        )

    return apply


def coupling(s, v_ref, j, mix_ref):
    return jnp.tanh(total(mix_ref[s, t] * v_ref[j, t] for t in range(v_ref.shape[1])))


def node_starts(s, points, fields, decay):
    for j, tau in enumerate(points):
        step = float(tau * time_step)
        shrink = 1.0 / (1.0 + step * decay)
        for start, force, v_ref in fields:
            v_ref[j, s] = (start + step * force) * shrink


def node_rates(s, v_ref, force, decay, mix_ref, apply):
    rows = v_ref.shape[2]
    out = []
    for j in range(v_ref.shape[0]):
        v = v_ref[j, s]
        moved = apply(v, pltpu.roll(v, rows - 1, 0), pltpu.roll(v, 1, 0), decay)
        out.append(moved + (coupling(s, v_ref, j, mix_ref) + force))
    return out


def swept(m, weights, points, rates, base, v, decay):
    count = len(rates)
    summed = total(float(time_step * weights[m, j]) * rates[j] for j in range(count))
    stiff = float(time_step * points[m] / count) * decay
    return (base + summed + stiff * v) / (1.0 + stiff)


def first_sweep(start_ref, before_ref, force_ref, force_before_ref, decay_ref, mix_ref, diff_ref,
                vel_ref, v_ref, w_ref, v1_ref, handed_ref, ready):
    species, rows, cells = start_ref.shape
    count = v_ref.shape[0]
    weights, points = quadrature(count)

    def begin(s, carry):
        decay = decay_ref[s]
        now = (start_ref[s], force_ref[s], v_ref)
        then = (before_ref[s], force_before_ref[s], w_ref)
        node_starts(s, points, (now, then), decay)
        return carry

    lax.fori_loop(0, species, begin, 0, unroll=4)

    ready()

    def sweep(s, carry):
        decay = decay_ref[s]
        apply = stencil(s, diff_ref, vel_ref, (rows, cells))
        rates = node_rates(s, v_ref, force_ref[s], decay, mix_ref, apply)
        for m in range(count):
            v1_ref[m, s] = swept(m, weights, points, rates, start_ref[s], v_ref[m, s], decay)
        return carry

    lax.fori_loop(0, species, sweep, 0, unroll=4)

    def sweep_before(s, carry):
        decay = decay_ref[s]
        apply = stencil(s, diff_ref, vel_ref, (rows, cells))
        m = count - 1
        row = [float(time_step * weights[m, j]) for j in range(count)]
        mixed = total(row[j] * w_ref[j, s] for j in range(count))
        coupled = total(row[j] * coupling(s, w_ref, j, mix_ref) for j in range(count))
        moved = apply(mixed, pltpu.roll(mixed, rows - 1, 0), pltpu.roll(mixed, 1, 0), decay)
        stiff = float(time_step * points[m] / count) * decay
        base = before_ref[s] + float(sum(row)) * force_before_ref[s]
        handed_ref[s] = (base + (moved + coupled) + stiff * w_ref[m, s]) / (1.0 + stiff)
        return carry

    lax.fori_loop(0, species, sweep_before, 0, unroll=4)


def fetch(sources, targets, sems):
    copies = [pltpu.make_async_copy(a, b, sems.at[i]) for i, (a, b) in enumerate(zip(sources, targets))]
    for copy in copies:
        copy.start()

    def ready():
        for copy in copies:
            copy.wait()

    return ready


def inner_kernel(start_ref, before_ref, force_ref, force_before_ref, decay_ref, mix_hbm, diff_hbm,
                 vel_hbm, v1_ref, handed_ref, v_ref, w_ref, mix_ref, diff_ref, vel_ref, sems):
    ready = fetch((mix_hbm, diff_hbm, vel_hbm), (mix_ref, diff_ref, vel_ref), sems)
    first_sweep(start_ref, before_ref, force_ref, force_before_ref, decay_ref, mix_ref, diff_ref,
                vel_ref, v_ref, w_ref, v1_ref, handed_ref, ready)


def start_kernel(place_ref, base_ref, gathered_ref, handover_ref, force_ref, decay_ref, mix_hbm, diff_hbm,
                 vel_hbm, start_ref, before_ref, force_before_ref, low_ref, high_ref):
    del mix_hbm, diff_hbm, vel_hbm
    member = place_ref[0]
    planes = base_ref.shape[1]
    for s in range(base_ref.shape[0]):
        base, decay = base_ref[s], decay_ref[s]
        grow = 1.0 + time_step * decay
        factor = 1.0 / grow
        start = base
        force_before = handover_ref[s]
        before = base * grow - time_step * force_before
        for k in range(TEAM - 1):
            passed = member > k
            force = gathered_ref[k, s]
            before = jnp.where(passed, start, before)
            force_before = jnp.where(passed, force, force_before)
            start = jnp.where(passed, factor * (start + time_step * force), start)
        start_ref[s] = start
        before_ref[s] = before
        force_before_ref[s] = force_before
        for k, field in enumerate((start, force_ref[s], decay)):
            low_ref[k, s] = field[:2]
            high_ref[k, s] = field[planes - 2 :]
        for k, field in enumerate((before, force_before)):
            low_ref[3, s, k : k + 1] = field[:1]
            high_ref[3, s, k : k + 1] = field[planes - 1 :]


def outer_kernel(place_ref, start_ref, before_ref, force_ref, force_before_ref, decay_ref,
                 initial_ref, below_ref, above_ref, v1_ref, handed_ref, mix_hbm, diff_hbm, vel_hbm,
                 out_ref, e_ref, v_ref, w_ref, v1e_ref, handede_ref, full_ref, mix_ref, diff_ref,
                 vel_ref, sems):
    ready = fetch((mix_hbm, diff_hbm, vel_hbm), (mix_ref, diff_ref, vel_ref), sems)
    node, slot, tile, tiles = place_ref[1], place_ref[2], place_ref[3], place_ref[4]
    species, planes, cells = start_ref.shape
    count = v_ref.shape[0]
    for k, ref in enumerate((start_ref, force_ref, decay_ref, before_ref, force_before_ref)):
        for s in range(species):
            if k < 3:
                e_ref[k, s, 0:2] = below_ref[k, s]
                e_ref[k, s, 6:8] = above_ref[k, s]
            else:
                for at in (0, 1):
                    e_ref[k, s, at : at + 1] = below_ref[3, s, k - 3 : k - 2]
                    e_ref[k, s, at + 6 : at + 7] = above_ref[3, s, k - 3 : k - 2]
            e_ref[k, s, 2:4] = ref[s, 0:2]
            e_ref[k, s, 4:6] = ref[s, planes - 2 : planes]
    first_sweep(e_ref.at[0], e_ref.at[3], e_ref.at[1], e_ref.at[4], e_ref.at[2], mix_ref, diff_ref,
                vel_ref, v_ref, w_ref, v1e_ref, handede_ref, ready)
    edge = lax.broadcasted_iota(jnp.int32, (8, cells), 0)
    outside = ((tile == 0) & (edge == 1)) | ((tile == tiles - 1) & (edge == 6))
    row = lax.broadcasted_iota(jnp.int32, (planes, cells), 0)

    def fill(s, carry):
        for j in range(count):
            v1e = v1e_ref[j, s]
            v1e_ref[j, s] = jnp.where(outside, 0.0, v1e)
            full_ref[j, s] = v1_ref[j, s]
            full_ref[j, s, 0:1] = v1e[2:3]
            full_ref[j, s, planes - 1 : planes] = v1e[5:6]
        return carry

    lax.fori_loop(0, species, fill, 0, unroll=4)
    weights = quadrature(count)[0]
    own_row = []
    for j in range(count):
        weight = jnp.float32(weights[0, j])
        for m in range(1, count):
            weight = jnp.where(node == m, jnp.float32(weights[m, j]), weight)
        own_row.append(weight)
    scale = float(time_step / count / count)
    stiff_of_node = scale * (node + 1).astype(jnp.float32)

    def finish(s, carry):
        decay = decay_ref[s]
        apply = stencil(s, diff_ref, vel_ref, (planes, cells))
        mixed = total(own_row[j] * full_ref[j, s] for j in range(count))
        mixed_edge = total(own_row[j] * v1e_ref[j, s] for j in range(count))
        x_plus = jnp.where(row == planes - 1, mixed_edge[6:7], pltpu.roll(mixed, planes - 1, 0))
        x_minus = jnp.where(row == 0, mixed_edge[1:2], pltpu.roll(mixed, 1, 0))
        coupled = total(own_row[j] * coupling(s, full_ref, j, mix_ref) for j in range(count))
        weight = total(own_row[j] for j in range(count))
        summed = apply(mixed, x_plus, x_minus, decay) + coupled + weight * force_ref[s]
        handede = handede_ref[s]
        handed = handed_ref[s]
        handed = jnp.where(row == 0, handede[2:3], handed)
        handed = jnp.where(row == planes - 1, handede[5:6], handed)
        second_start = jnp.where(slot == 0, initial_ref[s], handed)
        stiff = stiff_of_node * decay
        own = full_ref[node, s]
        out_ref[0, 0, s] = (second_start + time_step * summed + stiff * own) / (1.0 + stiff)
        return carry

    lax.fori_loop(0, species, finish, 0, unroll=4)


def call(kernel, outs, ins, scratch, cost, params=()):
    spaces = [{"s": pltpu.SMEM, "v": pltpu.VMEM, "h": pltpu.HBM}[kind] for kind in ins]
    scratch = [pltpu.VMEM(shape, jnp.float32) for shape in scratch]
    if params:
        scratch += [pltpu.SMEM(shape, jnp.float32) for shape in params]
        scratch += [pltpu.SemaphoreType.DMA((len(params),))]
    return pl.pallas_call(
        kernel,
        out_shape=[jax.ShapeDtypeStruct(shape, jnp.float32) for shape in outs],
        in_specs=[pl.BlockSpec(memory_space=space) for space in spaces],
        out_specs=[pl.BlockSpec(memory_space=pltpu.VMEM)] * len(outs),
        scratch_shapes=scratch,
        cost_estimate=pl.CostEstimate(flops=cost, bytes_accessed=cost // 8, transcendentals=0),
        compiler_params=pltpu.CompilerParams(vmem_limit_bytes=24 * 2**20),
    )


def team_base(initial, force, decay_rate):
    slices = lax.axis_size("tm")
    place = lax.axis_index("tm")
    member = place % TEAM
    team = place // TEAM
    teams = slices // TEAM
    groups = [[TEAM * g + i for i in range(TEAM)] for g in range(teams)]
    handover = lax.ppermute(force, "tm", [(TEAM * g - 1, TEAM * g) for g in range(1, teams)])
    gathered = lax.all_gather(force, "tm", axis_index_groups=groups)
    share = force.shape[0] // TEAM

    def own(array, axis):
        return lax.dynamic_slice_in_dim(array, member * share, share, axis)

    factor = 1.0 / (1.0 + time_step * own(decay_rate, 0))
    own_gathered = own(gathered, 1)
    summed = jnp.zeros_like(factor)
    for k in range(TEAM):
        summed = factor * (summed + time_step * own_gathered[k])
    factor2 = factor * factor
    factor4 = factor2 * factor2

    def send(value, *routes):
        pairs = [(TEAM * g + i, TEAM * t + i) for g, t in routes for i in range(TEAM)]
        return lax.ppermute(value, "tm", pairs)

    middle = teams // 2 - 1
    near = send(summed, *((g, g + 1) for g in range(middle + 1, teams - 1, 2)))
    state = own(initial, 0)
    for g in range(middle):
        arrived = send(factor4 * state + summed, (g, g + 1))
        state = jnp.where(team == g + 1, arrived, state)
    beside = []
    for g in range(middle, teams - 1, 2):
        ahead = factor4 * state + summed
        if g + 2 < teams:
            arrived = send(ahead, (g, g + 2))
            state = jnp.where(team == g + 2, factor4 * arrived + near, state)
        if g == middle:
            ahead = ahead + 0.0 * handover[:share]
        beside.append((g + 1, send(ahead, (g, g + 1))))
    for t, arrived in beside:
        state = jnp.where(team == t, arrived, state)
    base = lax.all_gather(state, "tm", axis=0, tiled=True, axis_index_groups=groups)
    return base, gathered, handover


def body(initial, forcing, decay_rate, mixing, diffusivity, velocity):
    count = lax.axis_size("node")
    node = lax.axis_index("node")
    place = lax.axis_index("tm")
    tiles = lax.axis_size("space")
    tile = lax.axis_index("space")
    force = forcing[0]
    base, gathered, handover = team_base(initial, force, decay_rate)
    where_am_i = jnp.stack([place % TEAM, node, place, tile, jnp.int32(tiles)]).astype(jnp.int32)
    full = force.shape
    params = (mixing, diffusivity, velocity)
    species, planes, cells = full
    edge = (4, species, 2, cells)
    start, before, force_before, low, high = call(
        start_kernel, [full, full, full, edge, edge], "svvvvvhhh", [], 2**20
    )(where_am_i, base, gathered, handover, force, decay_rate, *params)
    up = [(i, i + 1) for i in range(tiles - 1)]
    down = [(j, i) for i, j in up]
    below = lax.ppermute(high, "space", up)
    above = lax.ppermute(low, "space", down)
    nodes = (count,) + full
    shapes = [param.shape for param in params]
    fields = (start, before, force, force_before, decay_rate)
    v1, handed = call(inner_kernel, [nodes, full], "vvvvvhhh", [nodes, nodes], 2**25, shapes)(
        *fields, *params
    )
    small = (species, 8, cells)
    edges = (count,) + small
    (out,) = call(
        outer_kernel,
        [(1, 1) + full],
        "s" + "v" * 10 + "hhh",
        [(5,) + small, edges, edges, edges, small, nodes],
        2**25,
        shapes,
    )(where_am_i, *fields, initial, below, above, v1, handed, *params)
    return out


def solution(mesh):
    placed = (
        P(None, "space", None),
        P("tm", None, "space", None),
        P(None, "space", None),
        P(),
        P(),
        P(),
    )
    return jax.shard_map(
        body,
        mesh=mesh,
        in_specs=placed,
        out_specs=P("tm", "node", None, "space", None),
        check_vma=False,
    )
```

```python
import jax
import jax.numpy as jnp
import numpy as np
from jax import lax
from jax.experimental import pallas as pl
from jax.experimental.pallas import tpu as pltpu
from jax.sharding import PartitionSpec as P

NZ = 16
TEAM = 4
time_step = 0.05


def quadrature(node_count):
    points = [(position + 1.0) / node_count for position in range(node_count)]
    weights_table = np.zeros((node_count, node_count))
    for column in range(node_count):
        coeffs = [1.0]
        denominator = 1.0
        for other_node in range(node_count):
            if other_node != column:
                shifted = [0.0] + coeffs
                for degree in range(len(coeffs)):
                    shifted[degree] = shifted[degree] - points[other_node] * coeffs[degree]
                coeffs = shifted
                denominator = denominator * (points[column] - points[other_node])
        for row_node in range(node_count):
            running = 0.0
            for degree in range(len(coeffs)):
                running = running + coeffs[degree] * points[row_node] ** (degree + 1) / (degree + 1)
            weights_table[row_node, column] = running / denominator
    return (weights_table, np.array(points))


def total(terms):
    out = None
    for term in terms:
        out = term if out is None else out + term
    return out


def stencil(s, diff_ref, vel_ref, shape):
    rows, cells = shape
    d, vx, vy, vz = diff_ref[s], 0.5 * vel_ref[0, s], 0.5 * vel_ref[1, s], 0.5 * vel_ref[2, s]
    depth = lax.broadcasted_iota(jnp.int32, shape, 1) % NZ
    up = jnp.where(depth == NZ - 1, 0.0, d - vz)
    down = jnp.where(depth == 0, 0.0, d + vz)

    def apply(v, x_plus, x_minus, decay):
        y_plus = pltpu.roll(v, cells - NZ, 1)
        y_minus = pltpu.roll(v, NZ, 1)
        z_plus = pltpu.roll(v, cells - 1, 1)
        z_minus = pltpu.roll(v, 1, 1)
        return total(
            [
                (d - vx) * x_plus,
                (d + vx) * x_minus,
                (d - vy) * y_plus,
                (d + vy) * y_minus,
                up * z_plus,
                down * z_minus,
                (-6.0 * d - decay) * v,
            ]
        )

    return apply


def coupling(s, v_ref, j, mix_ref):
    return jnp.tanh(total(mix_ref[s, t] * v_ref[j, t] for t in range(v_ref.shape[1])))


def node_starts(s, points, fields, decay):
    for j, tau in enumerate(points):
        step = float(tau * time_step)
        shrink = 1.0 / (1.0 + step * decay)
        for start, force, v_ref in fields:
            v_ref[j, s] = (start + step * force) * shrink


def node_rates(s, v_ref, force, decay, mix_ref, apply):
    rows = v_ref.shape[2]
    out = []
    for j in range(v_ref.shape[0]):
        v = v_ref[j, s]
        moved = apply(v, pltpu.roll(v, rows - 1, 0), pltpu.roll(v, 1, 0), decay)
        out.append(moved + (coupling(s, v_ref, j, mix_ref) + force))
    return out


def swept(m, weights, points, rates, base, v, decay):
    count = len(rates)
    summed = total(float(time_step * weights[m, j]) * rates[j] for j in range(count))
    stiff = float(time_step * points[m] / count) * decay
    return (base + summed + stiff * v) / (1.0 + stiff)


def first_sweep(start_ref, before_ref, force_ref, force_before_ref, decay_ref, mix_ref, diff_ref,
                vel_ref, v_ref, w_ref, v1_ref, handed_ref, ready):
    species, rows, cells = start_ref.shape
    count = v_ref.shape[0]
    weights, points = quadrature(count)

    def begin(s, carry):
        decay = decay_ref[s]
        now = (start_ref[s], force_ref[s], v_ref)
        then = (before_ref[s], force_before_ref[s], w_ref)
        node_starts(s, points, (now, then), decay)
        return carry

    lax.fori_loop(0, species, begin, 0, unroll=8)

    ready()

    def sweep(s, carry):
        decay = decay_ref[s]
        apply = stencil(s, diff_ref, vel_ref, (rows, cells))
        rates = node_rates(s, v_ref, force_ref[s], decay, mix_ref, apply)
        for m in range(count):
            v1_ref[m, s] = swept(m, weights, points, rates, start_ref[s], v_ref[m, s], decay)
        return carry

    lax.fori_loop(0, species, sweep, 0, unroll=8)

    def sweep_before(s, carry):
        decay = decay_ref[s]
        apply = stencil(s, diff_ref, vel_ref, (rows, cells))
        m = count - 1
        row = [float(time_step * weights[m, j]) for j in range(count)]
        mixed = total(row[j] * w_ref[j, s] for j in range(count))
        coupled = total(row[j] * coupling(s, w_ref, j, mix_ref) for j in range(count))
        moved = apply(mixed, pltpu.roll(mixed, rows - 1, 0), pltpu.roll(mixed, 1, 0), decay)
        stiff = float(time_step * points[m] / count) * decay
        base = before_ref[s] + float(sum(row)) * force_before_ref[s]
        handed_ref[s] = (base + (moved + coupled) + stiff * w_ref[m, s]) / (1.0 + stiff)
        return carry

    lax.fori_loop(0, species, sweep_before, 0, unroll=8)


def fetch(sources, targets, sems):
    copies = [pltpu.make_async_copy(a, b, sems.at[i]) for i, (a, b) in enumerate(zip(sources, targets))]
    for copy in copies:
        copy.start()

    def ready():
        for copy in copies:
            copy.wait()

    return ready


def inner_kernel(start_ref, before_ref, force_ref, force_before_ref, decay_ref, mix_hbm, diff_hbm,
                 vel_hbm, v1_ref, handed_ref, v_ref, w_ref, mix_ref, diff_ref, vel_ref, sems):
    ready = fetch((mix_hbm, diff_hbm, vel_hbm), (mix_ref, diff_ref, vel_ref), sems)
    first_sweep(start_ref, before_ref, force_ref, force_before_ref, decay_ref, mix_ref, diff_ref,
                vel_ref, v_ref, w_ref, v1_ref, handed_ref, ready)


def start_kernel(place_ref, base_ref, gathered_ref, handover_ref, force_ref, decay_ref, mix_hbm, diff_hbm,
                 vel_hbm, start_ref, before_ref, force_before_ref, low_ref, high_ref):
    del mix_hbm, diff_hbm, vel_hbm
    member = place_ref[0]
    planes = base_ref.shape[1]
    for s in range(base_ref.shape[0]):
        base, decay = base_ref[s], decay_ref[s]
        grow = 1.0 + time_step * decay
        factor = 1.0 / grow
        start = base
        force_before = handover_ref[s]
        before = base * grow - time_step * force_before
        for k in range(TEAM - 1):
            passed = member > k
            force = gathered_ref[k, s]
            before = jnp.where(passed, start, before)
            force_before = jnp.where(passed, force, force_before)
            start = jnp.where(passed, factor * (start + time_step * force), start)
        start_ref[s] = start
        before_ref[s] = before
        force_before_ref[s] = force_before
        for k, field in enumerate((start, force_ref[s], decay)):
            low_ref[k, s] = field[:2]
            high_ref[k, s] = field[planes - 2 :]
        for k, field in enumerate((before, force_before)):
            low_ref[3, s, k : k + 1] = field[:1]
            high_ref[3, s, k : k + 1] = field[planes - 1 :]


def outer_kernel(place_ref, start_ref, before_ref, force_ref, force_before_ref, decay_ref,
                 initial_ref, below_ref, above_ref, v1_ref, handed_ref, mix_ref, diff_ref, vel_ref,
                 out_ref, e_ref, v_ref, w_ref, v1e_ref, handede_ref, full_ref):
    node, slot, tile, tiles = place_ref[1], place_ref[2], place_ref[3], place_ref[4]
    species, planes, cells = start_ref.shape
    count = v_ref.shape[0]
    for k, ref in enumerate((start_ref, force_ref, decay_ref, before_ref, force_before_ref)):
        for s in range(species):
            if k < 3:
                e_ref[k, s, 0:2] = below_ref[k, s]
                e_ref[k, s, 6:8] = above_ref[k, s]
            else:
                for at in (0, 1):
                    e_ref[k, s, at : at + 1] = below_ref[3, s, k - 3 : k - 2]
                    e_ref[k, s, at + 6 : at + 7] = above_ref[3, s, k - 3 : k - 2]
            e_ref[k, s, 2:4] = ref[s, 0:2]
            e_ref[k, s, 4:6] = ref[s, planes - 2 : planes]
    first_sweep(e_ref.at[0], e_ref.at[3], e_ref.at[1], e_ref.at[4], e_ref.at[2], mix_ref, diff_ref,
                vel_ref, v_ref, w_ref, v1e_ref, handede_ref, lambda: None)
    edge = lax.broadcasted_iota(jnp.int32, (8, cells), 0)
    outside = ((tile == 0) & (edge == 1)) | ((tile == tiles - 1) & (edge == 6))
    row = lax.broadcasted_iota(jnp.int32, (planes, cells), 0)

    def fill(s, carry):
        for j in range(count):
            v1e = v1e_ref[j, s]
            v1e_ref[j, s] = jnp.where(outside, 0.0, v1e)
            full_ref[j, s] = v1_ref[j, s]
            full_ref[j, s, 0:1] = v1e[2:3]
            full_ref[j, s, planes - 1 : planes] = v1e[5:6]
        return carry

    lax.fori_loop(0, species, fill, 0, unroll=8)
    weights = quadrature(count)[0]
    own_row = []
    for j in range(count):
        weight = jnp.float32(weights[0, j])
        for m in range(1, count):
            weight = jnp.where(node == m, jnp.float32(weights[m, j]), weight)
        own_row.append(weight)
    scale = float(time_step / count / count)
    stiff_of_node = scale * (node + 1).astype(jnp.float32)

    def finish(s, carry):
        decay = decay_ref[s]
        apply = stencil(s, diff_ref, vel_ref, (planes, cells))
        mixed = total(own_row[j] * full_ref[j, s] for j in range(count))
        mixed_edge = total(own_row[j] * v1e_ref[j, s] for j in range(count))
        x_plus = jnp.where(row == planes - 1, mixed_edge[6:7], pltpu.roll(mixed, planes - 1, 0))
        x_minus = jnp.where(row == 0, mixed_edge[1:2], pltpu.roll(mixed, 1, 0))
        coupled = total(own_row[j] * coupling(s, full_ref, j, mix_ref) for j in range(count))
        weight = total(own_row[j] for j in range(count))
        summed = apply(mixed, x_plus, x_minus, decay) + coupled + weight * force_ref[s]
        handede = handede_ref[s]
        handed = handed_ref[s]
        handed = jnp.where(row == 0, handede[2:3], handed)
        handed = jnp.where(row == planes - 1, handede[5:6], handed)
        second_start = jnp.where(slot == 0, initial_ref[s], handed)
        stiff = stiff_of_node * decay
        own = full_ref[node, s]
        out_ref[0, 0, s] = (second_start + time_step * summed + stiff * own) / (1.0 + stiff)
        return carry

    lax.fori_loop(0, species, finish, 0, unroll=8)


def call(kernel, outs, ins, scratch, cost, params=()):
    spaces = [{"s": pltpu.SMEM, "v": pltpu.VMEM, "h": pltpu.HBM}[kind] for kind in ins]
    scratch = [pltpu.VMEM(shape, jnp.float32) for shape in scratch]
    if params:
        scratch += [pltpu.SMEM(shape, jnp.float32) for shape in params]
        scratch += [pltpu.SemaphoreType.DMA((len(params),))]
    return pl.pallas_call(
        kernel,
        out_shape=[jax.ShapeDtypeStruct(shape, jnp.float32) for shape in outs],
        in_specs=[pl.BlockSpec(memory_space=space) for space in spaces],
        out_specs=[pl.BlockSpec(memory_space=pltpu.VMEM)] * len(outs),
        scratch_shapes=scratch,
        cost_estimate=pl.CostEstimate(flops=cost, bytes_accessed=cost // 8, transcendentals=0),
        compiler_params=pltpu.CompilerParams(vmem_limit_bytes=24 * 2**20),
    )


def team_base(initial, force, decay_rate):
    slices = lax.axis_size("tm")
    place = lax.axis_index("tm")
    member = place % TEAM
    team = place // TEAM
    teams = slices // TEAM
    groups = [[TEAM * g + i for i in range(TEAM)] for g in range(teams)]
    handover = lax.ppermute(force, "tm", [(TEAM * g - 1, TEAM * g) for g in range(1, teams)])
    gathered = lax.all_gather(force, "tm", axis_index_groups=groups)
    share = force.shape[0] // TEAM

    def own(array, axis):
        return lax.dynamic_slice_in_dim(array, member * share, share, axis)

    factor = 1.0 / (1.0 + time_step * own(decay_rate, 0))
    own_gathered = own(gathered, 1)
    summed = jnp.zeros_like(factor)
    for k in range(TEAM):
        summed = factor * (summed + time_step * own_gathered[k])
    factor2 = factor * factor
    factor4 = factor2 * factor2

    def send(value, *routes):
        pairs = [(TEAM * g + i, TEAM * t + i) for g, t in routes for i in range(TEAM)]
        return lax.ppermute(value, "tm", pairs)

    middle = teams // 2 - 1
    near = send(summed, *((g, g + 1) for g in range(middle + 1, teams - 1, 2)))
    state = own(initial, 0)
    for g in range(middle):
        arrived = send(factor4 * state + summed, (g, g + 1))
        state = jnp.where(team == g + 1, arrived, state)
    beside = []
    for g in range(middle, teams - 1, 2):
        ahead = factor4 * state + summed
        if g + 2 < teams:
            arrived = send(ahead, (g, g + 2))
            state = jnp.where(team == g + 2, factor4 * arrived + near, state)
        if g == middle:
            ahead = ahead + 0.0 * handover[:share]
        beside.append((g + 1, send(ahead, (g, g + 1))))
    for t, arrived in beside:
        state = jnp.where(team == t, arrived, state)
    base = lax.all_gather(state, "tm", axis=0, tiled=True, axis_index_groups=groups)
    return base, gathered, handover


def body(initial, forcing, decay_rate, mixing, diffusivity, velocity):
    count = lax.axis_size("node")
    node = lax.axis_index("node")
    place = lax.axis_index("tm")
    tiles = lax.axis_size("space")
    tile = lax.axis_index("space")
    force = forcing[0]
    base, gathered, handover = team_base(initial, force, decay_rate)
    where_am_i = jnp.stack([place % TEAM, node, place, tile, jnp.int32(tiles)]).astype(jnp.int32)
    full = force.shape
    params = (mixing, diffusivity, velocity)
    species, planes, cells = full
    edge = (4, species, 2, cells)
    start, before, force_before, low, high = call(
        start_kernel, [full, full, full, edge, edge], "svvvvvhhh", [], 2**20
    )(where_am_i, base, gathered, handover, force, decay_rate, *params)
    up = [(i, i + 1) for i in range(tiles - 1)]
    down = [(j, i) for i, j in up]
    below = lax.ppermute(high, "space", up)
    above = lax.ppermute(low, "space", down)
    nodes = (count,) + full
    shapes = [param.shape for param in params]
    fields = (start, before, force, force_before, decay_rate)
    v1, handed = call(inner_kernel, [nodes, full], "vvvvvhhh", [nodes, nodes], 2**25, shapes)(
        *fields, *params
    )
    small = (species, 8, cells)
    edges = (count,) + small
    (out,) = call(
        outer_kernel,
        [(1, 1) + full],
        "s" + "v" * 10 + "sss",
        [(5,) + small, edges, edges, edges, small, nodes],
        2**25,
    )(where_am_i, *fields, initial, below, above, v1, handed, *params)
    return out


def solution(mesh):
    placed = (
        P(None, "space", None),
        P("tm", None, "space", None),
        P(None, "space", None),
        P(),
        P(),
        P(),
    )
    return jax.shard_map(
        body,
        mesh=mesh,
        in_specs=placed,
        out_specs=P("tm", "node", None, "space", None),
        check_vma=False,
    )
```
